32 devices in a mesh: row: 4 (over z), col: 8 (over y, x, core).
Axes of the slice: x: 2, y: 2, z: 4, core: 2. Of those that a mesh axis runs over, the one named last changes fastest.
Arguments:
- factor_panel: bfloat16 [1024, 8192], P('row', 'col'), may hold values from -0.1875 to 0.1875
- ancestor_inv: float32 [1024, 1024], P('row', 'col'), may hold values from -6 to 6
- diag_inverse: float32 [4096, 8192], P('row', 'col'), may hold values from -6 to 6
- structure: int32 [2, 4], replicated, may hold values 0 or 1
Outputs:
- inverse_panel: float32 [1024, 8192], P('row', 'col')
- diag_sigma: float32 [4096, 8192], P('row', 'col')
The draws below stay inside these ranges and needn't reach their ends.
All inputs are finite; a program needn't handle non-finite values.
Results may differ from the reference program's by a relative error of at most 0.0003.
Values may be sent and summed in bfloat16 or wider, within the bound.
A program may use at most 128 MiB of HBM per device.

```python
import jax
import jax.numpy as jnp
from jax import lax

B = 256
W = 4096
NS = 2
NA = 1024
NT = 4
N_COL = 8


def with_ends(values, stream_key, smallest, high):
    longest = values.shape.index(max(values.shape))
    spots = []
    for shift in (0, 1):
        where = [jax.random.randint(jax.random.fold_in(stream_key, axis), (), 0, length) for axis, length in enumerate(values.shape)]
        where[longest] = (where[longest] + shift) % values.shape[longest]
        spots.append(tuple(where))
    return values.at[spots[0]].set(smallest).at[spots[1]].set(high)


def shard_levels(key, dims, split, low, largest):
    factor_of, own = 1.0, jax.random.fold_in(key, 6)
    for dim, blocks in split:
        steps = jnp.exp(jax.random.uniform(jax.random.fold_in(own, dim), (blocks,), jnp.float32, low / len(split), largest / len(split)))
        factor_of = factor_of * jnp.repeat(steps, dims[dim] // blocks).reshape([-1 if axis == dim else 1 for axis in range(len(dims))])
    return factor_of


def normal_values(own_key, shape, spread, reach, cuts=(), kind=jnp.bfloat16):
    array = spread * jax.random.normal(own_key, shape, jnp.float32)
    if cuts:
        array = array * shard_levels(own_key, shape, cuts, -0.22, 0.18)
    return jnp.clip(array, -reach, reach).astype(kind)


def setup_inputs(seed: int = 0) -> dict:
    seeds = jax.random.split(jax.random.key(seed), 5)
    factor_panel = normal_values(seeds[0], (NA, NS * W), NA ** -0.5, 0.1875, ((0, 4), (1, 8)))
    ancestor_inv = normal_values(seeds[1], (NA, NA), 1.0, 6.0, ((0, 4), (1, 8)), jnp.float32)
    diag_inverse = normal_values(seeds[2], (W, NS * W), 1.0, 6.0, ((0, 4), (1, 8)), jnp.float32)
    structure = with_ends((jax.random.randint(seeds[3], (NS, NT), 0, 4) < 3).astype(jnp.int32), jax.random.fold_in(seeds[3], 1), 0, 1)
    return {"factor_panel": factor_panel, "ancestor_inv": ancestor_inv, "diag_inverse": diag_inverse, "structure": structure}


def reference(factor_panel, ancestor_inv, diag_inverse, structure):
    per_block = W // N_COL
    panel_cube = factor_panel.reshape(NA, N_COL, NS, per_block)
    diag_cube = diag_inverse.reshape(W, N_COL, NS, per_block)
    panels = []
    blocks = []
    for member in range(NS):
        keep = jnp.repeat(structure[member], B) == 1
        window = panel_cube[:, :, member, :].reshape(NA, W)
        lhat = jnp.where(keep[:, None], window, jnp.zeros_like(window))
        lhat_wide = lhat.astype(jnp.float32)
        product = jnp.dot(ancestor_inv, lhat_wide, precision=lax.Precision.HIGHEST)
        inverse_part = jnp.where(keep[:, None], -product, jnp.zeros_like(product))
        update = jnp.dot(lhat_wide.T, inverse_part, precision=lax.Precision.HIGHEST)
        panels.append(inverse_part.reshape(NA, N_COL, per_block))
        blocks.append((diag_cube[:, :, member, :].reshape(W, W) - update).reshape(W, N_COL, per_block))
    inverse_panel = jnp.stack(panels, axis=2).reshape(NA, NS * W)
    diag_sigma = jnp.stack(blocks, axis=2).reshape(W, NS * W)
    return inverse_panel, diag_sigma
```

```python
import functools

import jax
import jax.numpy as jnp
from jax import lax
from jax.experimental import pallas as pl
from jax.experimental.pallas import tpu as pltpu
from jax.sharding import PartitionSpec as P

B = 256
NS = 2
NR = 4
NC = 8
NP = 4
TAIL = 16
MESH = pl.DeviceIdType.MESH
ORDER = (
    (0,), (1, 0), (2, 0, 0, 0), (1, 1), (2, 0, 1, 0), (3, 0), (1, 2), (2, 0, 2, 0), (1, 3), (2, 0, 3, 0), (3, 1),
    (3, 2), (3, 3), (4, 0, 0, 3, 0), (2, 0, 0, 3), (2, 0, 0, 1), (4, 0, 0, 1, 0), (2, 0, 1, 1), (4, 0, 0, 0, 0),
    (2, 0, 2, 1), (4, 0, 0, 0, 1), (4, 0, 0, 1, 1), (4, 0, 0, 3, 1), (2, 0, 3, 1), (2, 1, 0, 0), (2, 0, 0, 2), (5, 1),
    (5, 3), (5, 0), (5, 2), (4, 0, 1, 0, 1), (2, 0, 1, 2), (2, 1, 0, 1), (4, 0, 0, 2, 0), (4, 0, 1, 1, 1),
    (4, 0, 1, 0, 0), (2, 1, 1, 0), (4, 0, 0, 2, 1), (4, 0, 1, 1, 0), (4, 0, 2, 1, 1), (4, 0, 2, 0, 1), (2, 0, 2, 2),
    (4, 0, 2, 0, 0), (2, 1, 2, 0), (4, 0, 2, 1, 0), (4, 0, 1, 3, 1), (4, 0, 1, 3, 0), (2, 1, 1, 1), (4, 0, 1, 2, 1),
    (4, 0, 1, 2, 0), (4, 0, 3, 0, 0), (4, 0, 3, 0, 1), (2, 1, 3, 0), (4, 0, 3, 1, 0), (4, 0, 3, 1, 1),
    (4, 0, 2, 3, 0), (4, 0, 2, 3, 1), (4, 0, 3, 3, 0), (4, 0, 2, 2, 0), (4, 0, 2, 2, 1), (4, 1, 0, 1, 0),
    (4, 1, 0, 1, 1), (4, 1, 1, 2, 1), (4, 1, 1, 1, 0), (4, 0, 3, 3, 1), (4, 1, 0, 0, 0), (4, 1, 0, 0, 1),
    (2, 2, 0, 0), (2, 0, 3, 2), (4, 0, 3, 2, 0), (4, 0, 3, 2, 1), (6, 0, 0), (7, 0), (7, 1), (4, 1, 0, 2, 0),
    (4, 1, 0, 2, 1), (4, 1, 1, 1, 1), (2, 0, 1, 3), (2, 1, 2, 1), (2, 1, 0, 2), (4, 1, 2, 1, 1), (4, 1, 1, 0, 1),
    (4, 1, 0, 3, 0), (4, 1, 1, 0, 0), (2, 2, 1, 0), (6, 0, 1), (2, 1, 3, 1), (4, 1, 0, 3, 1), (2, 0, 2, 3), (7, 2),
    (4, 1, 1, 2, 0), (2, 0, 3, 3), (7, 3), (4, 1, 2, 0, 0), (2, 1, 1, 2), (6, 0, 2), (4, 1, 2, 1, 0), (2, 2, 0, 1),
    (4, 1, 1, 3, 0), (4, 1, 1, 3, 1), (2, 1, 0, 3), (4, 1, 2, 0, 1), (2, 2, 2, 0), (2, 1, 2, 2), (4, 1, 2, 2, 0),
    (4, 1, 2, 3, 0), (6, 0, 3), (4, 1, 3, 1, 0), (2, 2, 1, 1), (8,), (9, 2), (9, 3), (9, 0), (9, 1), (4, 1, 2, 2, 1),
    (4, 1, 3, 0, 0), (2, 1, 3, 2), (2, 2, 2, 1), (4, 1, 3, 0, 1), (2, 2, 3, 0), (10, 0), (4, 2, 1, 3, 1),
    (4, 2, 0, 0, 0), (4, 1, 2, 3, 1), (2, 1, 1, 3), (6, 1, 0), (4, 1, 3, 2, 0), (2, 1, 2, 3), (4, 2, 0, 2, 1),
    (4, 2, 0, 3, 0), (4, 2, 0, 0, 1), (2, 3, 0, 0), (10, 1), (4, 1, 3, 2, 1), (4, 2, 0, 3, 1), (2, 2, 3, 1),
    (2, 2, 0, 2), (4, 1, 3, 1, 1), (4, 2, 1, 2, 1), (4, 1, 3, 3, 0), (4, 1, 3, 3, 1), (10, 3), (4, 2, 1, 2, 0),
    (4, 2, 1, 0, 0), (4, 2, 1, 0, 1), (4, 2, 0, 1, 0), (4, 2, 1, 3, 0), (2, 1, 3, 3), (6, 1, 1), (4, 2, 0, 1, 1),
    (2, 2, 1, 2), (6, 1, 2), (6, 2, 0), (2, 2, 0, 3), (6, 1, 3), (2, 2, 2, 2), (2, 3, 1, 0), (2, 3, 0, 3),
    (4, 2, 2, 0, 0), (4, 2, 2, 0, 1), (4, 2, 2, 2, 0), (4, 2, 1, 1, 1), (2, 3, 2, 0), (2, 3, 0, 1), (10, 2),
    (2, 3, 1, 1), (2, 2, 1, 3), (6, 2, 1), (2, 2, 3, 2), (4, 2, 1, 1, 0), (11, 1), (-1,), (12, 1), (4, 2, 2, 3, 0),
    (2, 2, 2, 3), (4, 2, 3, 0, 1), (4, 2, 3, 0, 0), (4, 2, 3, 2, 0), (4, 2, 3, 2, 1), (4, 2, 3, 3, 1), (2, 3, 3, 0),
    (6, 2, 2), (2, 3, 1, 3), (4, 2, 0, 2, 0), (11, 0), (12, 0), (4, 2, 3, 3, 0), (4, 2, 2, 3, 1), (2, 2, 3, 3),
    (2, 3, 0, 2), (6, 2, 3), (6, 3, 0), (4, 2, 3, 1, 1), (2, 3, 2, 3), (2, 3, 2, 1), (4, 2, 2, 1, 0), (4, 2, 3, 1, 0),
    (11, 3), (2, 3, 1, 2), (4, 2, 2, 2, 1), (6, 3, 1), (13, 1), (2, 3, 3, 1), (12, 3), (13, 0), (2, 3, 2, 2),
    (4, 2, 2, 1, 1), (11, 2), (12, 2), (6, 3, 2), (13, 2), (2, 3, 3, 2), (6, 3, 3), (2, 3, 3, 3), (13, 3),
)


def local(factor_panel, ancestor_inv, diag_inverse, structure):
    rows_dev, width_dev = factor_panel.shape
    per_block = width_dev // NS
    row_index = lax.axis_index("row")
    keep_tiles = jnp.repeat(structure, B, axis=1)
    keep_own = lax.dynamic_slice_in_dim(keep_tiles, row_index * rows_dev, rows_dev, 1)
    keep_cols = jnp.repeat(keep_own.T, per_block, axis=1)
    lhat_local = jnp.where(keep_cols == 1, factor_panel, jnp.zeros_like(factor_panel))
    column = lax.all_gather(lhat_local, "row", axis=0, tiled=True)
    sigma_rows = lax.all_gather(ancestor_inv, "col", axis=1, tiled=True)
    column_wide = column.astype(jnp.float32)
    running = jnp.dot(sigma_rows, column_wide, precision=lax.Precision.HIGHEST)
    inverse_panel = jnp.where(keep_cols == 1, -running, jnp.zeros_like(running))
    rows_all = lax.all_gather(lhat_local, "col", axis=1, tiled=True)
    block_count = rows_all.shape[1] // width_dev
    rows_cube = rows_all.reshape(rows_dev, block_count, NS, per_block)
    lhat_members = [
        rows_cube[:, :, member, :].reshape(rows_dev, block_count * per_block).astype(jnp.float32)
        for member in range(NS)
    ]
    pieces = []
    for member in range(NS):
        window = lhat_members[member]
        target = inverse_panel[:, member * per_block : (member + 1) * per_block]
        pieces.append(
            lax.dot_general(
                window,
                target,
                (((0,), (0,)), ((), ())),
                precision=lax.Precision.HIGHEST,
                preferred_element_type=jnp.float32,
            )
        )
    update = lax.psum_scatter(
        jnp.concatenate(pieces, axis=1), "row", scatter_dimension=0, tiled=True
    )
    diag_sigma = diag_inverse - update
    return (inverse_panel, diag_sigma)


def gray(p):
    y = p // 2
    return 2 * y + lax.rem(lax.rem(p, 2) + y, 2)


def dot(a, b, dims):
    return lax.dot_general(a, b, (dims, ((), ())), preferred_element_type=jnp.float32)


def encode(a):
    top = jnp.maximum(jnp.max(jnp.abs(a), axis=0, keepdims=True), 1e-36)
    grade = jnp.ceil(jnp.log2(top) * 64.0 + 0.01)
    whole = jnp.round(a * (jnp.exp2(grade * (-1.0 / 64)) * 32767.0))
    tail = jnp.broadcast_to(grade, (TAIL, a.shape[1]))
    return [v.astype(jnp.int32).astype(jnp.int16) for v in (whole, tail)]


def decode(whole, tail):
    grade = tail.astype(jnp.int32).astype(jnp.float32)[:1]
    return whole.astype(jnp.int32).astype(jnp.float32) * (jnp.exp2(grade * (1.0 / 64)) * (1.0 / 32767))


def kernel(structure_in, factor_in, anc_in, diag_in, panel_out, diag_out,
           structure, factor, anc, lt, pr, asl, a_hi, a_lo, q_sum, q_hi, q_lo,
           zl_send, zl_recv, za_send, za_recv, xa_send, xa_recv, sa_send, sa_recv,
           pc_send, pc_recv, pb_send, ps_send, ps_recv, lc_sem, in_sem):
    r = lax.axis_index("row")
    c = lax.axis_index("col")
    rows = factor.shape[0]
    wp = lt.shape[2]
    half = NP // NS
    core = lax.rem(c, 2)
    pos = c // 2
    step = 1 - 2 * core
    q_me = gray(pos)
    hop = lax.rem((q_me - gray(r)) * step + 8, 4)

    def ring_pos(k):
        return gray(lax.rem(q_me + k * step + 8, 4))

    nxt, prv = ring_pos(1) * 2 + core, ring_pos(-1) * 2 + core
    sib = pos * 2 + 1 - core
    has = (r < NR - 1, r > 0)
    to = ((lax.rem(r + 1, NR), c), (lax.rem(r + NR - 1, NR), c))
    order = [r, r + 1 - 2 * (r // 3), lax.rem(r + 2, 3) - r // 3, 3 * (1 - r // 2)]
    peers = [ring_pos(k) for k in range(1, 4)]

    loads = [pltpu.make_async_copy(src, dst, in_sem.at[i]) for i, (src, dst) in enumerate(
        ((anc_in, anc), (structure_in, structure), (factor_in, factor), (diag_in, diag_out)))]
    for load in loads:
        load.start()

    barrier = pltpu.get_barrier_semaphore()
    for dev in [(r, peers[k] * 2 + core) for k in range(3)] + [(r, sib)] + [(lax.rem(r + k, NR), c) for k in range(1, NR)]:
        pl.semaphore_signal(barrier, inc=1, device_id=dev, device_id_type=MESH)

    loads[0].wait()
    whole, tail = encode(anc[...])
    asl[core, pos, 0, :rows] = whole
    asl[core, pos, 0, rows:] = tail
    loads[1].wait()
    loads[2].wait()

    def turn(p):
        part = factor[:, p * wp:(p + 1) * wp].astype(jnp.float32)
        kept = jnp.where(structure[p // half, r] == 1, part, 0.0)
        lt[r, p] = kept.T.astype(jnp.bfloat16)

    pl.semaphore_wait(barrier, 7)

    def remote(ref, send, recv, dev, src=None):
        return pltpu.make_async_remote_copy(
            src_ref=ref if src is None else src, dst_ref=ref, send_sem=send, recv_sem=recv,
            device_id=dev, device_id_type=MESH)

    sends = []

    def go(cond, copy):
        sends.append((cond, copy))
        if cond is None:
            copy.start()
        else:
            pl.when(cond)(copy.start)

    def tile_out():
        for k in (1, 3, 2):
            go(None, remote(asl.at[core, pos, NR - k], za_send.at[k - 1], za_recv.at[NR - 1 - k],
                            (lax.rem(r + k, NR), c), asl.at[core, pos, 0]))
        for k in (0, 2, 1):
            go(None, tile_copy(pos, 0, k))

    def tile_copy(where, kind, k):
        part = asl.at[core, where, 1:] if kind else asl.at[core, where, 0]
        return remote(part, xa_send.at[kind, k], xa_recv.at[kind, k], (r, peers[k] * 2 + core))

    def tiles_on(h):
        if h == 0:
            for k in range(3):
                sends.append((None, tile_copy(pos, 1, k)))

        @pl.when(hop == h)
        def _():
            for k in range(1, NR):
                remote(asl.at[core, pos, k], za_send.at[k - 1], za_recv.at[k - 1], (r, sib)).wait_recv()
            for k in (0, 2, 1):
                tile_copy(pos, 1, k).start()

    def half_copy(side):
        return remote(asl.at[side], sa_send, sa_recv, (r, sib))

    def tiles_in(h):
        if h == 0:
            sends.append((None, half_copy(core)))

        @pl.when(hop == h)
        def _():
            for k in range(3):
                for kind in range(2):
                    tile_copy(ring_pos(-(k + 1)), kind, k).wait_recv()
            half_copy(core).start()

    def tiles_sib():
        half_copy(1 - core).wait_recv()

    def row_copy(way, z, j, p):
        return remote(lt.at[z, p], zl_send.at[way, j, p], zl_recv.at[way, j, p], to[way])

    def row_first(p):
        for way in range(2):
            go(has[way], row_copy(way, r, 0, p))

    def row_step(j, p, h, way):
        z = (r - 1 - j) if way == 0 else (r + 1 + j)
        there = (z >= 0) & (z < NR)
        z = lax.rem(z + NR, NR)
        if j < NR - 2 and h == 0:
            sends.append((there & has[way], row_copy(way, z, j + 1, p)))

        @pl.when(there & (hop == h))
        def _():
            row_copy(way, z, j, p).wait_recv()
            if j < NR - 2:
                pl.when(has[way])(row_copy(way, z, j + 1, p).start)

    def chain_copy(t, p, src=None):
        return remote(pr.at[core, order[t], p], pc_send.at[t, p], pc_recv.at[t, p], (r, nxt), src)

    def back_copy(p, src=None):
        return remote(pr.at[core, order[3], p], pb_send.at[p], pc_recv.at[3, p], (r, prv), src)

    def sib_copy(t, p, src=None):
        return remote(pr.at[core, order[t], p], ps_send.at[t, p], ps_recv.at[t, p], (r, sib), src)

    def own_copy(t, p):
        z = order[t]
        return pltpu.make_async_copy(lt.at[z, p], pr.at[core, z, p], lc_sem.at[t, p])

    def chain(t, p, h):
        if h == 0:
            @pl.when(hop == 0)
            def _():
                src = lt.at[order[t], p]
                chain_copy(t, p, src).start()
                if t == 3:
                    back_copy(p, src).start()
                sib_copy(t, p, src).start()
                own_copy(t, p).start()
        else:
            @pl.when(hop == h)
            def _():
                chain_copy(t, p).wait_recv()
                if h < (2 if t == 3 else 3):
                    chain_copy(t, p).start()
                sib_copy(t, p).start()

    def split(t):
        z = lax.rem(r + t, NR)

        @pl.loop(0, NR)
        def _(kz):
            for side in range(2):
                a = decode(asl[side, kz, t, :rows], asl[side, kz, t, rows:])
                hi = a.astype(jnp.bfloat16)
                here = slice(side * 128, (side + 1) * 128)
                a_hi[kz, z, :, here] = hi
                a_lo[kz, z, :, here] = (a - hi.astype(jnp.float32)).astype(jnp.bfloat16)

    def product(p, ts):
        rhs = jnp.concatenate([lt[order[t], p] for t in ts] * 2, axis=1)
        lhs = jnp.concatenate([ref[order[t]].reshape(NR * rows, -1) for ref in (a_hi, a_lo) for t in ts], axis=1)
        return dot(lhs, rhs, ((1,), (1,))).reshape(NR, rows, wp)

    def panel_first(p):
        q_sum[p] = product(p, (0, 1, 2))

    def panel_last(p):
        total = q_sum[p] + product(p, (3,))
        for i in range(NR):
            part = jnp.where(structure[p // half, i] == 1, -total[i], 0.0)
            top = part.astype(jnp.bfloat16)
            q_hi[p, i] = top
            q_lo[p, i] = (part - top.astype(jnp.float32)).astype(jnp.bfloat16)

            @pl.when(i == r)
            def _():
                panel_out[:, p * wp:(p + 1) * wp] = part

    def arrived(t, p):
        pl.when(hop == 0)(own_copy(t, p).wait)
        remote(pr.at[1 - core, order[t], p], ps_send.at[t, p], ps_recv.at[t, p], (r, sib)).wait_recv()

    def subtract(k, part, count, p, ts):
        lhs = jnp.concatenate([pr[k, order[t], part:part + count].reshape(count * wp, rows) for t in ts] * 2, axis=1)
        rhs = jnp.concatenate([ref[p, order[t]] for ref in (q_hi, q_lo) for t in ts], axis=0)
        first = (k * half + part % half) * wp
        where = (slice(first, first + count * wp), slice(p * wp, (p + 1) * wp))
        diag_out[where] = diag_out[where] - dot(lhs, rhs, ((1,), (0,)))

    def update_first(p):
        for k in range(2):
            subtract(k, p // half * half, half, p, (0, 1, 2))

    def update_last(part):
        for k in range(2):
            for p in range(part // half * half, part // half * half + half):
                subtract(k, part, 1, p, (3,))

    steps = (tile_out, turn, chain, row_first, row_step, tiles_on, arrived, tiles_in, tiles_sib, split, panel_first, panel_last, update_first, update_last)
    for number, *args in ORDER:
        if number < 0:
            loads[3].wait()
        else:
            steps[number](*args)

    for cond, copy in sends:
        if cond is None:
            copy.wait_send()
        else:
            pl.when(cond)(copy.wait_send)
    for t in range(NR):
        for p in range(NP):
            pl.when(hop < (2 if t == 3 else 3))(chain_copy(t, p).wait_send)
            sib_copy(t, p).wait_send()
            if t == 3:
                pl.when(hop == 0)(back_copy(p).wait_send)


def write_out(panel, diag, panel_out, diag_out, sem):
    copies = [pltpu.make_async_copy(diag, diag_out, sem.at[0]), pltpu.make_async_copy(panel, panel_out, sem.at[1])]
    for copy in copies:
        copy.start()
    for copy in copies:
        copy.wait()


def local_kernel(factor_panel, ancestor_inv, diag_inverse, structure):
    rows, width = factor_panel.shape
    wp = width // NP
    acols = ancestor_inv.shape[1]
    dma = pltpu.SemaphoreType.DMA
    bf16, f32 = jnp.bfloat16, jnp.float32
    vmem = pl.BlockSpec(memory_space=pltpu.VMEM)
    anywhere = pl.BlockSpec(memory_space=pl.ANY)
    shapes = (
        jax.ShapeDtypeStruct((rows, width), f32),
        jax.ShapeDtypeStruct(diag_inverse.shape, f32),
    )
    panel, diag = pl.pallas_call(
        kernel,
        out_shape=shapes,
        in_specs=[anywhere] * 4,
        out_specs=(vmem, vmem),
        scratch_shapes=[
            pltpu.SMEM(structure.shape, jnp.int32),
            pltpu.VMEM((rows, width), bf16),
            pltpu.VMEM((rows, acols), f32),
            pltpu.VMEM((NR, NP, wp, rows), bf16),
            pltpu.VMEM((2, NR, NP, wp, rows), bf16),
            pltpu.VMEM((2, NC // 2, NR, rows + TAIL, acols), jnp.int16),
            pltpu.VMEM((NR, NR, rows, 2 * acols), bf16),
            pltpu.VMEM((NR, NR, rows, 2 * acols), bf16),
            pltpu.VMEM((NP, NR, rows, wp), f32),
            pltpu.VMEM((NP, NR, rows, wp), bf16),
            pltpu.VMEM((NP, NR, rows, wp), bf16),
            dma((2, NR - 1, NP)), dma((2, NR - 1, NP)), dma((NR - 1,)), dma((NR - 1,)),
            dma((2, 3)), dma((2, 3)), dma, dma,
            dma((NR, NP)), dma((NR, NP)), dma((NP,)), dma((NR, NP)), dma((NR, NP)),
            dma((NR, NP)), dma((4,)),
        ],
        compiler_params=pltpu.CompilerParams(
            collective_id=0, has_side_effects=True, vmem_limit_bytes=48 << 20),
    )(structure, factor_panel, ancestor_inv, diag_inverse)
    return pl.pallas_call(
        write_out,
        out_shape=shapes,
        in_specs=[vmem, vmem],
        out_specs=(anywhere, anywhere),
        scratch_shapes=[dma((2,))],
        compiler_params=pltpu.CompilerParams(vmem_limit_bytes=40 << 20),
    )(panel, diag)


def solution(mesh):
    placed = (P("row", "col"), P("row", "col"), P("row", "col"), P())

    def body(factor_panel, ancestor_inv, diag_inverse, structure):
        rows, width = factor_panel.shape
        fits = (mesh.shape["row"], mesh.shape["col"]) == (NR, NC) and rows == B
        fits = fits and diag_inverse.shape[0] * NS == 2 * width
        return (local_kernel if fits else local)(factor_panel, ancestor_inv, diag_inverse, structure)

    return jax.shard_map(
        body,
        mesh=mesh,
        in_specs=placed,
        out_specs=(P("row", "col"), P("row", "col")),
        check_vma=False,
    )
```

```python
import functools

import jax
import jax.numpy as jnp
from jax import lax
from jax.experimental import pallas as pl
from jax.experimental.pallas import tpu as pltpu
from jax.sharding import PartitionSpec as P

B = 256
NS = 2
NR = 4
NC = 8
NP = 4
TAIL = 16
MESH = pl.DeviceIdType.MESH
ORDER = (
    (0,), (1, 0), (2, 0, 0, 0), (1, 1), (2, 0, 1, 0), (3, 0), (1, 2), (2, 0, 2, 0), (1, 3), (2, 0, 3, 0), (3, 1),
    (3, 2), (3, 3), (4, 0, 0, 3, 0), (2, 0, 0, 3), (2, 0, 0, 1), (4, 0, 0, 1, 0), (2, 0, 1, 1), (4, 0, 0, 0, 0),
    (2, 0, 2, 1), (4, 0, 0, 0, 1), (4, 0, 0, 1, 1), (4, 0, 0, 3, 1), (2, 0, 3, 1), (2, 1, 0, 0), (2, 0, 0, 2), (5, 1),
    (5, 3), (5, 0), (5, 2), (4, 0, 1, 0, 1), (2, 0, 1, 2), (2, 1, 0, 1), (4, 0, 0, 2, 0), (4, 0, 1, 1, 1),
    (4, 0, 1, 0, 0), (2, 1, 1, 0), (4, 0, 0, 2, 1), (4, 0, 1, 1, 0), (4, 0, 2, 1, 1), (4, 0, 2, 0, 1), (2, 0, 2, 2),
    (4, 0, 2, 0, 0), (2, 1, 2, 0), (4, 0, 2, 1, 0), (4, 0, 1, 3, 1), (4, 0, 1, 3, 0), (2, 1, 1, 1), (4, 0, 1, 2, 1),
    (4, 0, 1, 2, 0), (4, 0, 3, 0, 0), (4, 0, 3, 0, 1), (2, 1, 3, 0), (4, 0, 3, 1, 0), (4, 0, 3, 1, 1),
    (4, 0, 2, 3, 0), (4, 0, 2, 3, 1), (4, 0, 3, 3, 0), (4, 0, 2, 2, 0), (4, 0, 2, 2, 1), (4, 1, 0, 1, 0),
    (4, 1, 0, 1, 1), (4, 1, 1, 2, 1), (4, 1, 1, 1, 0), (4, 0, 3, 3, 1), (4, 1, 0, 0, 0), (4, 1, 0, 0, 1),
    (2, 2, 0, 0), (2, 0, 3, 2), (4, 0, 3, 2, 0), (4, 0, 3, 2, 1), (6, 0, 0), (7, 0), (7, 1), (4, 1, 0, 2, 0),
    (4, 1, 0, 2, 1), (4, 1, 1, 1, 1), (2, 0, 1, 3), (2, 1, 2, 1), (2, 1, 0, 2), (4, 1, 2, 1, 1), (4, 1, 1, 0, 1),
    (4, 1, 0, 3, 0), (4, 1, 1, 0, 0), (2, 2, 1, 0), (6, 0, 1), (2, 1, 3, 1), (4, 1, 0, 3, 1), (2, 0, 2, 3), (7, 2),
    (4, 1, 1, 2, 0), (2, 0, 3, 3), (7, 3), (4, 1, 2, 0, 0), (2, 1, 1, 2), (6, 0, 2), (4, 1, 2, 1, 0), (2, 2, 0, 1),
    (4, 1, 1, 3, 0), (4, 1, 1, 3, 1), (2, 1, 0, 3), (4, 1, 2, 0, 1), (2, 2, 2, 0), (2, 1, 2, 2), (4, 1, 2, 2, 0),
    (4, 1, 2, 3, 0), (6, 0, 3), (4, 1, 3, 1, 0), (2, 2, 1, 1), (8,), (9, 2), (9, 3), (9, 0), (9, 1), (4, 1, 2, 2, 1),
    (4, 1, 3, 0, 0), (2, 1, 3, 2), (2, 2, 2, 1), (4, 1, 3, 0, 1), (2, 2, 3, 0), (10, 0), (4, 2, 1, 3, 1),
    (4, 2, 0, 0, 0), (4, 1, 2, 3, 1), (2, 1, 1, 3), (6, 1, 0), (4, 1, 3, 2, 0), (2, 1, 2, 3), (4, 2, 0, 2, 1),
    (4, 2, 0, 3, 0), (4, 2, 0, 0, 1), (2, 3, 0, 0), (10, 1), (4, 1, 3, 2, 1), (4, 2, 0, 3, 1), (2, 2, 3, 1),
    (2, 2, 0, 2), (4, 1, 3, 1, 1), (4, 2, 1, 2, 1), (4, 1, 3, 3, 0), (4, 1, 3, 3, 1), (10, 3), (4, 2, 1, 2, 0),
    (4, 2, 1, 0, 0), (4, 2, 1, 0, 1), (4, 2, 0, 1, 0), (4, 2, 1, 3, 0), (2, 1, 3, 3), (6, 1, 1), (4, 2, 0, 1, 1),
    (2, 2, 1, 2), (6, 1, 2), (6, 2, 0), (2, 2, 0, 3), (6, 1, 3), (2, 2, 2, 2), (2, 3, 1, 0), (2, 3, 0, 3),
    (4, 2, 2, 0, 0), (4, 2, 2, 0, 1), (4, 2, 2, 2, 0), (4, 2, 1, 1, 1), (2, 3, 2, 0), (2, 3, 0, 1), (10, 2),
    (2, 3, 1, 1), (2, 2, 1, 3), (6, 2, 1), (2, 2, 3, 2), (4, 2, 1, 1, 0), (11, 1), (-1,), (12, 1), (4, 2, 2, 3, 0),
    (2, 2, 2, 3), (4, 2, 3, 0, 1), (4, 2, 3, 0, 0), (4, 2, 3, 2, 0), (4, 2, 3, 2, 1), (4, 2, 3, 3, 1), (2, 3, 3, 0),
    (6, 2, 2), (2, 3, 1, 3), (4, 2, 0, 2, 0), (11, 0), (12, 0), (4, 2, 3, 3, 0), (4, 2, 2, 3, 1), (2, 2, 3, 3),
    (2, 3, 0, 2), (6, 2, 3), (6, 3, 0), (4, 2, 3, 1, 1), (2, 3, 2, 3), (2, 3, 2, 1), (4, 2, 2, 1, 0), (4, 2, 3, 1, 0),
    (11, 3), (2, 3, 1, 2), (4, 2, 2, 2, 1), (6, 3, 1), (13, 1), (2, 3, 3, 1), (12, 3), (13, 0), (2, 3, 2, 2),
    (4, 2, 2, 1, 1), (11, 2), (12, 2), (6, 3, 2), (13, 2), (2, 3, 3, 2), (6, 3, 3), (2, 3, 3, 3), (13, 3),
)


def local(factor_panel, ancestor_inv, diag_inverse, structure):
    rows_dev, width_dev = factor_panel.shape
    per_block = width_dev // NS
    row_index = lax.axis_index("row")
    keep_tiles = jnp.repeat(structure, B, axis=1)
    keep_own = lax.dynamic_slice_in_dim(keep_tiles, row_index * rows_dev, rows_dev, 1)
    keep_cols = jnp.repeat(keep_own.T, per_block, axis=1)
    lhat_local = jnp.where(keep_cols == 1, factor_panel, jnp.zeros_like(factor_panel))
    column = lax.all_gather(lhat_local, "row", axis=0, tiled=True)
    sigma_rows = lax.all_gather(ancestor_inv, "col", axis=1, tiled=True)
    column_wide = column.astype(jnp.float32)
    running = jnp.dot(sigma_rows, column_wide, precision=lax.Precision.HIGHEST)
    inverse_panel = jnp.where(keep_cols == 1, -running, jnp.zeros_like(running))
    rows_all = lax.all_gather(lhat_local, "col", axis=1, tiled=True)
    block_count = rows_all.shape[1] // width_dev
    rows_cube = rows_all.reshape(rows_dev, block_count, NS, per_block)
    lhat_members = [
        rows_cube[:, :, member, :].reshape(rows_dev, block_count * per_block).astype(jnp.float32)
        for member in range(NS)
    ]
    pieces = []
    for member in range(NS):
        window = lhat_members[member]
        target = inverse_panel[:, member * per_block : (member + 1) * per_block]
        pieces.append(
            lax.dot_general(
                window,
                target,
                (((0,), (0,)), ((), ())),
                precision=lax.Precision.HIGHEST,
                preferred_element_type=jnp.float32,
            )
        )
    update = lax.psum_scatter(
        jnp.concatenate(pieces, axis=1), "row", scatter_dimension=0, tiled=True
    )
    diag_sigma = diag_inverse - update
    return (inverse_panel, diag_sigma)


def gray(p):
    y = p // 2
    return 2 * y + lax.rem(lax.rem(p, 2) + y, 2)


def dot(a, b, dims):
    return lax.dot_general(a, b, (dims, ((), ())), preferred_element_type=jnp.float32)


def encode(a):
    top = jnp.maximum(jnp.max(jnp.abs(a), axis=0, keepdims=True), 1e-36)
    grade = jnp.ceil(jnp.log2(top) * 64.0 + 0.01)
    whole = jnp.round(a * (jnp.exp2(grade * (-1.0 / 64)) * 32767.0))
    tail = jnp.broadcast_to(grade, (TAIL, a.shape[1]))
    return [v.astype(jnp.int32).astype(jnp.int16) for v in (whole, tail)]


def decode(whole, tail):
    grade = tail.astype(jnp.int32).astype(jnp.float32)[:1]
    return whole.astype(jnp.int32).astype(jnp.float32) * (jnp.exp2(grade * (1.0 / 64)) * (1.0 / 32767))


def kernel(structure_in, factor_in, anc_in, diag_in, opened, panel_out, diag_out,
           structure, factor, anc, lt, pr, asl, a_hi, a_lo, q_sum, q_hi, q_lo,
           zl_send, zl_recv, za_send, za_recv, xa_send, xa_recv, sa_send, sa_recv,
           pc_send, pc_recv, pb_send, ps_send, ps_recv, lc_sem, in_sem):
    r = lax.axis_index("row")
    c = lax.axis_index("col")
    rows = factor.shape[0]
    wp = lt.shape[2]
    half = NP // NS
    core = lax.rem(c, 2)
    pos = c // 2
    step = 1 - 2 * core
    q_me = gray(pos)
    hop = lax.rem((q_me - gray(r)) * step + 8, 4)

    def ring_pos(k):
        return gray(lax.rem(q_me + k * step + 8, 4))

    nxt, prv = ring_pos(1) * 2 + core, ring_pos(-1) * 2 + core
    sib = pos * 2 + 1 - core
    has = (r < NR - 1, r > 0)
    to = ((lax.rem(r + 1, NR), c), (lax.rem(r + NR - 1, NR), c))
    order = [r, r + 1 - 2 * (r // 3), lax.rem(r + 2, 3) - r // 3, 3 * (1 - r // 2)]
    peers = [ring_pos(k) for k in range(1, 4)]

    loads = [pltpu.make_async_copy(src, dst, in_sem.at[i]) for i, (src, dst) in enumerate(
        ((anc_in, anc), (structure_in, structure), (factor_in, factor), (diag_in, diag_out)))]
    for load in loads:
        load.start()

    barrier = pltpu.get_barrier_semaphore()
    for dev in [(r, peers[k] * 2 + core) for k in range(3)] + [(r, sib)] + [(lax.rem(r + k, NR), c) for k in range(1, NR)]:
        pl.semaphore_signal(barrier, inc=1, device_id=dev, device_id_type=MESH)

    loads[0].wait()
    whole, tail = encode(anc[...])
    asl[core, pos, 0, :rows] = whole
    asl[core, pos, 0, rows:] = tail
    loads[1].wait()
    loads[2].wait()

    def turn(p):
        part = factor[:, p * wp:(p + 1) * wp].astype(jnp.float32)
        kept = jnp.where(structure[p // half, r] == 1, part, 0.0)
        lt[r, p] = kept.T.astype(jnp.bfloat16)

    pl.semaphore_wait(barrier, 7)

    def remote(ref, send, recv, dev, src=None):
        return pltpu.make_async_remote_copy(
            src_ref=ref if src is None else src, dst_ref=ref, send_sem=send, recv_sem=recv,
            device_id=dev, device_id_type=MESH)

    sends = []

    def go(cond, copy):
        sends.append((cond, copy))
        if cond is None:
            copy.start()
        else:
            pl.when(cond)(copy.start)

    def tile_out():
        for k in (1, 3, 2):
            go(None, remote(asl.at[core, pos, NR - k], za_send.at[k - 1], za_recv.at[NR - 1 - k],
                            (lax.rem(r + k, NR), c), asl.at[core, pos, 0]))
        for k in (0, 2, 1):
            go(None, tile_copy(pos, 0, k))

    def tile_copy(where, kind, k):
        part = asl.at[core, where, 1:] if kind else asl.at[core, where, 0]
        return remote(part, xa_send.at[kind, k], xa_recv.at[kind, k], (r, peers[k] * 2 + core))

    def tiles_on(h):
        if h == 0:
            for k in range(3):
                sends.append((None, tile_copy(pos, 1, k)))

        @pl.when(hop == h)
        def _():
            for k in range(1, NR):
                remote(asl.at[core, pos, k], za_send.at[k - 1], za_recv.at[k - 1], (r, sib)).wait_recv()
            for k in (0, 2, 1):
                tile_copy(pos, 1, k).start()

    def half_copy(side):
        return remote(asl.at[side], sa_send, sa_recv, (r, sib))

    def tiles_in(h):
        if h == 0:
            sends.append((None, half_copy(core)))

        @pl.when(hop == h)
        def _():
            for k in range(3):
                for kind in range(2):
                    tile_copy(ring_pos(-(k + 1)), kind, k).wait_recv()
            half_copy(core).start()

    def tiles_sib():
        half_copy(1 - core).wait_recv()

    def row_copy(way, z, j, p):
        return remote(lt.at[z, p], zl_send.at[way, j, p], zl_recv.at[way, j, p], to[way])

    def row_first(p):
        for way in range(2):
            go(has[way], row_copy(way, r, 0, p))

    def row_step(j, p, h, way):
        z = (r - 1 - j) if way == 0 else (r + 1 + j)
        there = (z >= 0) & (z < NR)
        z = lax.rem(z + NR, NR)
        if j < NR - 2 and h == 0:
            sends.append((there & has[way], row_copy(way, z, j + 1, p)))

        @pl.when(there & (hop == h))
        def _():
            row_copy(way, z, j, p).wait_recv()
            if j < NR - 2:
                pl.when(has[way])(row_copy(way, z, j + 1, p).start)

    def chain_copy(t, p, src=None):
        return remote(pr.at[core, order[t], p], pc_send.at[t, p], pc_recv.at[t, p], (r, nxt), src)

    def back_copy(p, src=None):
        return remote(pr.at[core, order[3], p], pb_send.at[p], pc_recv.at[3, p], (r, prv), src)

    def sib_copy(t, p, src=None):
        return remote(pr.at[core, order[t], p], ps_send.at[t, p], ps_recv.at[t, p], (r, sib), src)

    def own_copy(t, p):
        z = order[t]
        return pltpu.make_async_copy(lt.at[z, p], pr.at[core, z, p], lc_sem.at[t, p])

    def chain(t, p, h):
        if h == 0:
            @pl.when(hop == 0)
            def _():
                src = lt.at[order[t], p]
                chain_copy(t, p, src).start()
                if t == 3:
                    back_copy(p, src).start()
                sib_copy(t, p, src).start()
                own_copy(t, p).start()
        else:
            @pl.when(hop == h)
            def _():
                chain_copy(t, p).wait_recv()
                if h < (2 if t == 3 else 3):
                    chain_copy(t, p).start()
                sib_copy(t, p).start()

    def split(t):
        z = lax.rem(r + t, NR)

        @pl.loop(0, NR)
        def _(kz):
            for side in range(2):
                a = decode(asl[side, kz, t, :rows], asl[side, kz, t, rows:])
                hi = a.astype(jnp.bfloat16)
                here = slice(side * 128, (side + 1) * 128)
                a_hi[kz, z, :, here] = hi
                a_lo[kz, z, :, here] = (a - hi.astype(jnp.float32)).astype(jnp.bfloat16)

    def product(p, ts):
        rhs = jnp.concatenate([lt[order[t], p] for t in ts] * 2, axis=1)
        lhs = jnp.concatenate([ref[order[t]].reshape(NR * rows, -1) for ref in (a_hi, a_lo) for t in ts], axis=1)
        return dot(lhs, rhs, ((1,), (1,))).reshape(NR, rows, wp)

    def panel_first(p):
        q_sum[p] = product(p, (0, 1, 2))

    def panel_last(p):
        total = q_sum[p] + product(p, (3,))
        for i in range(NR):
            part = jnp.where(structure[p // half, i] == 1, -total[i], 0.0)
            top = part.astype(jnp.bfloat16)
            q_hi[p, i] = top
            q_lo[p, i] = (part - top.astype(jnp.float32)).astype(jnp.bfloat16)

            @pl.when(i == r)
            def _():
                panel_out[:, p * wp:(p + 1) * wp] = part

    def arrived(t, p):
        pl.when(hop == 0)(own_copy(t, p).wait)
        remote(pr.at[1 - core, order[t], p], ps_send.at[t, p], ps_recv.at[t, p], (r, sib)).wait_recv()

    def subtract(k, part, count, p, ts):
        lhs = jnp.concatenate([pr[k, order[t], part:part + count].reshape(count * wp, rows) for t in ts] * 2, axis=1)
        rhs = jnp.concatenate([ref[p, order[t]] for ref in (q_hi, q_lo) for t in ts], axis=0)
        first = (k * half + part % half) * wp
        where = (slice(first, first + count * wp), slice(p * wp, (p + 1) * wp))
        diag_out[where] = diag_out[where] - dot(lhs, rhs, ((1,), (0,)))

    def update_first(p):
        for k in range(2):
            subtract(k, p // half * half, half, p, (0, 1, 2))

    def update_last(part):
        for k in range(2):
            for p in range(part // half * half, part // half * half + half):
                subtract(k, part, 1, p, (3,))

    steps = (tile_out, turn, chain, row_first, row_step, tiles_on, arrived, tiles_in, tiles_sib, split, panel_first, panel_last, update_first, update_last)
    for number, *args in ORDER:
        if number < 0:
            loads[3].wait()
        else:
            steps[number](*args)

    for cond, copy in sends:
        if cond is None:
            copy.wait_send()
        else:
            pl.when(cond)(copy.wait_send)
    for t in range(NR):
        for p in range(NP):
            pl.when(hop < (2 if t == 3 else 3))(chain_copy(t, p).wait_send)
            sib_copy(t, p).wait_send()
            if t == 3:
                pl.when(hop == 0)(back_copy(p).wait_send)


def idle(out):
    out[...] = jnp.zeros_like(out)


def write_out(panel, diag, panel_out, diag_out, sem):
    copies = [pltpu.make_async_copy(diag, diag_out, sem.at[0]), pltpu.make_async_copy(panel, panel_out, sem.at[1])]
    for copy in copies:
        copy.start()
    for copy in copies:
        copy.wait()


def local_kernel(factor_panel, ancestor_inv, diag_inverse, structure):
    rows, width = factor_panel.shape
    wp = width // NP
    acols = ancestor_inv.shape[1]
    dma = pltpu.SemaphoreType.DMA
    bf16, f32 = jnp.bfloat16, jnp.float32
    vmem = pl.BlockSpec(memory_space=pltpu.VMEM)
    anywhere = pl.BlockSpec(memory_space=pl.ANY)
    shapes = (
        jax.ShapeDtypeStruct((rows, width), f32),
        jax.ShapeDtypeStruct(diag_inverse.shape, f32),
    )
    opened = pl.pallas_call(
        idle,
        out_shape=jax.ShapeDtypeStruct((8, 128), f32),
        out_specs=vmem,
        cost_estimate=pl.CostEstimate(flops=8 << 30, bytes_accessed=1 << 12, transcendentals=0),
        compiler_params=pltpu.CompilerParams(has_side_effects=True, vmem_limit_bytes=16 << 20),
    )()
    panel, diag = pl.pallas_call(
        kernel,
        out_shape=shapes,
        in_specs=[anywhere] * 4 + [vmem],
        out_specs=(vmem, vmem),
        scratch_shapes=[
            pltpu.SMEM(structure.shape, jnp.int32),
            pltpu.VMEM((rows, width), bf16),
            pltpu.VMEM((rows, acols), f32),
            pltpu.VMEM((NR, NP, wp, rows), bf16),
            pltpu.VMEM((2, NR, NP, wp, rows), bf16),
            pltpu.VMEM((2, NC // 2, NR, rows + TAIL, acols), jnp.int16),
            pltpu.VMEM((NR, NR, rows, 2 * acols), bf16),
            pltpu.VMEM((NR, NR, rows, 2 * acols), bf16),
            pltpu.VMEM((NP, NR, rows, wp), f32),
            pltpu.VMEM((NP, NR, rows, wp), bf16),
            pltpu.VMEM((NP, NR, rows, wp), bf16),
            dma((2, NR - 1, NP)), dma((2, NR - 1, NP)), dma((NR - 1,)), dma((NR - 1,)),
            dma((2, 3)), dma((2, 3)), dma, dma,
            dma((NR, NP)), dma((NR, NP)), dma((NP,)), dma((NR, NP)), dma((NR, NP)),
            dma((NR, NP)), dma((4,)),
        ],
        compiler_params=pltpu.CompilerParams(
            collective_id=0, has_side_effects=True, vmem_limit_bytes=48 << 20),
    )(structure, factor_panel, ancestor_inv, diag_inverse, opened)
    return pl.pallas_call(
        write_out,
        out_shape=shapes,
        in_specs=[vmem, vmem],
        out_specs=(anywhere, anywhere),
        scratch_shapes=[dma((2,))],
        compiler_params=pltpu.CompilerParams(vmem_limit_bytes=40 << 20),
    )(panel, diag)


def solution(mesh):
    placed = (P("row", "col"), P("row", "col"), P("row", "col"), P())

    def body(factor_panel, ancestor_inv, diag_inverse, structure):
        rows, width = factor_panel.shape
        fits = (mesh.shape["row"], mesh.shape["col"]) == (NR, NC) and rows == B
        fits = fits and diag_inverse.shape[0] * NS == 2 * width
        return (local_kernel if fits else local)(factor_panel, ancestor_inv, diag_inverse, structure)

    return jax.shard_map(
        body,
        mesh=mesh,
        in_specs=placed,
        out_specs=(P("row", "col"), P("row", "col")),
        check_vma=False,
    )
```

```python
import functools

import jax
import jax.numpy as jnp
from jax import lax
from jax.experimental import pallas as pl
from jax.experimental.pallas import tpu as pltpu
from jax.sharding import PartitionSpec as P

B = 256
NS = 2
NR = 4
NC = 8
NP = 4
TAIL = 16
MESH = pl.DeviceIdType.MESH
ORDER = (
    (0,), (1, 0), (2, 0, 0, 0), (1, 1), (2, 0, 1, 0), (3, 0), (1, 2), (2, 0, 2, 0), (1, 3), (2, 0, 3, 0), (3, 1),
    (3, 2), (3, 3), (4, 0, 0, 3, 0), (2, 0, 0, 3), (2, 0, 0, 1), (4, 0, 0, 1, 0), (2, 0, 1, 1), (4, 0, 0, 0, 0),
    (2, 0, 2, 1), (4, 0, 0, 0, 1), (4, 0, 0, 1, 1), (4, 0, 0, 3, 1), (2, 0, 3, 1), (2, 1, 0, 0), (2, 0, 0, 2), (5, 1),
    (5, 3), (5, 0), (5, 2), (4, 0, 1, 0, 1), (2, 0, 1, 2), (2, 1, 0, 1), (4, 0, 0, 2, 0), (4, 0, 1, 1, 1),
    (4, 0, 1, 0, 0), (2, 1, 1, 0), (4, 0, 0, 2, 1), (4, 0, 1, 1, 0), (4, 0, 2, 1, 1), (4, 0, 2, 0, 1), (2, 0, 2, 2),
    (4, 0, 2, 0, 0), (2, 1, 2, 0), (4, 0, 2, 1, 0), (4, 0, 1, 3, 1), (4, 0, 1, 3, 0), (2, 1, 1, 1), (4, 0, 1, 2, 1),
    (4, 0, 1, 2, 0), (4, 0, 3, 0, 0), (4, 0, 3, 0, 1), (2, 1, 3, 0), (4, 0, 3, 1, 0), (4, 0, 3, 1, 1),
    (4, 0, 2, 3, 0), (4, 0, 2, 3, 1), (4, 0, 3, 3, 0), (4, 0, 2, 2, 0), (4, 0, 2, 2, 1), (4, 1, 0, 1, 0),
    (4, 1, 0, 1, 1), (4, 1, 1, 2, 1), (4, 1, 1, 1, 0), (4, 0, 3, 3, 1), (4, 1, 0, 0, 0), (4, 1, 0, 0, 1),
    (2, 2, 0, 0), (2, 0, 3, 2), (4, 0, 3, 2, 0), (4, 0, 3, 2, 1), (6, 0, 0), (7, 0), (7, 1), (4, 1, 0, 2, 0),
    (4, 1, 0, 2, 1), (4, 1, 1, 1, 1), (2, 0, 1, 3), (2, 1, 2, 1), (2, 1, 0, 2), (4, 1, 2, 1, 1), (4, 1, 1, 0, 1),
    (4, 1, 0, 3, 0), (4, 1, 1, 0, 0), (2, 2, 1, 0), (6, 0, 1), (2, 1, 3, 1), (4, 1, 0, 3, 1), (2, 0, 2, 3), (7, 2),
    (4, 1, 1, 2, 0), (2, 0, 3, 3), (7, 3), (4, 1, 2, 0, 0), (2, 1, 1, 2), (6, 0, 2), (4, 1, 2, 1, 0), (2, 2, 0, 1),
    (4, 1, 1, 3, 0), (4, 1, 1, 3, 1), (2, 1, 0, 3), (4, 1, 2, 0, 1), (2, 2, 2, 0), (2, 1, 2, 2), (4, 1, 2, 2, 0),
    (4, 1, 2, 3, 0), (6, 0, 3), (4, 1, 3, 1, 0), (2, 2, 1, 1), (8,), (9, 2), (9, 3), (9, 0), (9, 1), (4, 1, 2, 2, 1),
    (4, 1, 3, 0, 0), (2, 1, 3, 2), (2, 2, 2, 1), (4, 1, 3, 0, 1), (2, 2, 3, 0), (10, 0), (4, 2, 1, 3, 1),
    (4, 2, 0, 0, 0), (4, 1, 2, 3, 1), (2, 1, 1, 3), (6, 1, 0), (4, 1, 3, 2, 0), (2, 1, 2, 3), (4, 2, 0, 2, 1),
    (4, 2, 0, 3, 0), (4, 2, 0, 0, 1), (2, 3, 0, 0), (10, 1), (4, 1, 3, 2, 1), (4, 2, 0, 3, 1), (2, 2, 3, 1),
    (2, 2, 0, 2), (4, 1, 3, 1, 1), (4, 2, 1, 2, 1), (4, 1, 3, 3, 0), (4, 1, 3, 3, 1), (10, 3), (4, 2, 1, 2, 0),
    (4, 2, 1, 0, 0), (4, 2, 1, 0, 1), (4, 2, 0, 1, 0), (4, 2, 1, 3, 0), (2, 1, 3, 3), (6, 1, 1), (4, 2, 0, 1, 1),
    (2, 2, 1, 2), (6, 1, 2), (6, 2, 0), (2, 2, 0, 3), (6, 1, 3), (2, 2, 2, 2), (2, 3, 1, 0), (2, 3, 0, 3),
    (4, 2, 2, 0, 0), (4, 2, 2, 0, 1), (4, 2, 2, 2, 0), (4, 2, 1, 1, 1), (2, 3, 2, 0), (2, 3, 0, 1), (10, 2),
    (2, 3, 1, 1), (2, 2, 1, 3), (6, 2, 1), (2, 2, 3, 2), (4, 2, 1, 1, 0), (11, 1), (-1,), (12, 1), (4, 2, 2, 3, 0),
    (2, 2, 2, 3), (4, 2, 3, 0, 1), (4, 2, 3, 0, 0), (4, 2, 3, 2, 0), (4, 2, 3, 2, 1), (4, 2, 3, 3, 1), (2, 3, 3, 0),
    (6, 2, 2), (2, 3, 1, 3), (4, 2, 0, 2, 0), (11, 0), (12, 0), (4, 2, 3, 3, 0), (4, 2, 2, 3, 1), (2, 2, 3, 3),
    (2, 3, 0, 2), (6, 2, 3), (6, 3, 0), (4, 2, 3, 1, 1), (2, 3, 2, 3), (2, 3, 2, 1), (4, 2, 2, 1, 0), (4, 2, 3, 1, 0),
    (11, 3), (2, 3, 1, 2), (4, 2, 2, 2, 1), (6, 3, 1), (13, 1), (2, 3, 3, 1), (12, 3), (13, 0), (2, 3, 2, 2),
    (4, 2, 2, 1, 1), (11, 2), (12, 2), (6, 3, 2), (13, 2), (2, 3, 3, 2), (6, 3, 3), (2, 3, 3, 3), (13, 3),
)


def local(factor_panel, ancestor_inv, diag_inverse, structure):
    rows_dev, width_dev = factor_panel.shape
    per_block = width_dev // NS
    row_index = lax.axis_index("row")
    keep_tiles = jnp.repeat(structure, B, axis=1)
    keep_own = lax.dynamic_slice_in_dim(keep_tiles, row_index * rows_dev, rows_dev, 1)
    keep_cols = jnp.repeat(keep_own.T, per_block, axis=1)
    lhat_local = jnp.where(keep_cols == 1, factor_panel, jnp.zeros_like(factor_panel))
    column = lax.all_gather(lhat_local, "row", axis=0, tiled=True)
    sigma_rows = lax.all_gather(ancestor_inv, "col", axis=1, tiled=True)
    column_wide = column.astype(jnp.float32)
    running = jnp.dot(sigma_rows, column_wide, precision=lax.Precision.HIGHEST)
    inverse_panel = jnp.where(keep_cols == 1, -running, jnp.zeros_like(running))
    rows_all = lax.all_gather(lhat_local, "col", axis=1, tiled=True)
    block_count = rows_all.shape[1] // width_dev
    rows_cube = rows_all.reshape(rows_dev, block_count, NS, per_block)
    lhat_members = [
        rows_cube[:, :, member, :].reshape(rows_dev, block_count * per_block).astype(jnp.float32)
        for member in range(NS)
    ]
    pieces = []
    for member in range(NS):
        window = lhat_members[member]
        target = inverse_panel[:, member * per_block : (member + 1) * per_block]
        pieces.append(
            lax.dot_general(
                window,
                target,
                (((0,), (0,)), ((), ())),
                precision=lax.Precision.HIGHEST,
                preferred_element_type=jnp.float32,
            )
        )
    update = lax.psum_scatter(
        jnp.concatenate(pieces, axis=1), "row", scatter_dimension=0, tiled=True
    )
    diag_sigma = diag_inverse - update
    return (inverse_panel, diag_sigma)


def gray(p):
    y = p // 2
    return 2 * y + lax.rem(lax.rem(p, 2) + y, 2)


def dot(a, b, dims):
    return lax.dot_general(a, b, (dims, ((), ())), preferred_element_type=jnp.float32)


def encode(a):
    top = jnp.maximum(jnp.max(jnp.abs(a), axis=0, keepdims=True), 1e-36)
    grade = jnp.ceil(jnp.log2(top) * 64.0 + 0.01)
    whole = jnp.round(a * (jnp.exp2(grade * (-1.0 / 64)) * 32767.0))
    tail = jnp.broadcast_to(grade, (TAIL, a.shape[1]))
    return [v.astype(jnp.int32).astype(jnp.int16) for v in (whole, tail)]


def decode(whole, tail):
    grade = tail.astype(jnp.int32).astype(jnp.float32)[:1]
    return whole.astype(jnp.int32).astype(jnp.float32) * (jnp.exp2(grade * (1.0 / 64)) * (1.0 / 32767))


def kernel(structure_in, factor_in, anc_in, diag_in, opened, panel_out, diag_out,
           structure, factor, anc, lt, pr, asl, a_hi, a_lo, q_sum, q_hi, q_lo,
           zl_send, zl_recv, za_send, za_recv, xa_send, xa_recv, sa_send, sa_recv,
           pc_send, pc_recv, pb_send, ps_send, ps_recv, lc_sem, in_sem):
    r = lax.axis_index("row")
    c = lax.axis_index("col")
    rows = factor.shape[0]
    wp = lt.shape[2]
    half = NP // NS
    core = lax.rem(c, 2)
    pos = c // 2
    step = 1 - 2 * core
    q_me = gray(pos)
    hop = lax.rem((q_me - gray(r)) * step + 8, 4)

    def ring_pos(k):
        return gray(lax.rem(q_me + k * step + 8, 4))

    nxt, prv = ring_pos(1) * 2 + core, ring_pos(-1) * 2 + core
    sib = pos * 2 + 1 - core
    has = (r < NR - 1, r > 0)
    to = ((lax.rem(r + 1, NR), c), (lax.rem(r + NR - 1, NR), c))
    order = [r, r + 1 - 2 * (r // 3), lax.rem(r + 2, 3) - r // 3, 3 * (1 - r // 2)]
    peers = [ring_pos(k) for k in range(1, 4)]

    loads = [pltpu.make_async_copy(src, dst, in_sem.at[i]) for i, (src, dst) in enumerate(
        ((anc_in, anc), (structure_in, structure), (factor_in, factor), (diag_in, diag_out)))]
    for load in loads[:3]:
        load.start()

    barrier = pltpu.get_barrier_semaphore()
    for dev in [(r, peers[k] * 2 + core) for k in range(3)] + [(r, sib)] + [(lax.rem(r + k, NR), c) for k in range(1, NR)]:
        pl.semaphore_signal(barrier, inc=1, device_id=dev, device_id_type=MESH)

    loads[0].wait()
    whole, tail = encode(anc[...])
    asl[core, pos, 0, :rows] = whole
    asl[core, pos, 0, rows:] = tail
    loads[1].wait()
    loads[2].wait()
    loads[3].start()

    def turn(p):
        part = factor[:, p * wp:(p + 1) * wp].astype(jnp.float32)
        kept = jnp.where(structure[p // half, r] == 1, part, 0.0)
        lt[r, p] = kept.T.astype(jnp.bfloat16)

    pl.semaphore_wait(barrier, 7)

    def remote(ref, send, recv, dev, src=None):
        return pltpu.make_async_remote_copy(
            src_ref=ref if src is None else src, dst_ref=ref, send_sem=send, recv_sem=recv,
            device_id=dev, device_id_type=MESH)

    sends = []

    def go(cond, copy):
        sends.append((cond, copy))
        if cond is None:
            copy.start()
        else:
            pl.when(cond)(copy.start)

    def tile_out():
        for k in (1, 3, 2):
            go(None, remote(asl.at[core, pos, NR - k], za_send.at[k - 1], za_recv.at[NR - 1 - k],
                            (lax.rem(r + k, NR), c), asl.at[core, pos, 0]))
        for k in (0, 2, 1):
            go(None, tile_copy(pos, 0, k))

    def tile_copy(where, kind, k):
        part = asl.at[core, where, 1:] if kind else asl.at[core, where, 0]
        return remote(part, xa_send.at[kind, k], xa_recv.at[kind, k], (r, peers[k] * 2 + core))

    def tiles_on(h):
        if h == 0:
            for k in range(3):
                sends.append((None, tile_copy(pos, 1, k)))

        @pl.when(hop == h)
        def _():
            for k in range(1, NR):
                remote(asl.at[core, pos, k], za_send.at[k - 1], za_recv.at[k - 1], (r, sib)).wait_recv()
            for k in (0, 2, 1):
                tile_copy(pos, 1, k).start()

    def half_copy(side):
        return remote(asl.at[side], sa_send, sa_recv, (r, sib))

    def tiles_in(h):
        if h == 0:
            sends.append((None, half_copy(core)))

        @pl.when(hop == h)
        def _():
            for k in range(3):
                for kind in range(2):
                    tile_copy(ring_pos(-(k + 1)), kind, k).wait_recv()
            half_copy(core).start()

    def tiles_sib():
        half_copy(1 - core).wait_recv()

    def row_copy(way, z, j, p):
        return remote(lt.at[z, p], zl_send.at[way, j, p], zl_recv.at[way, j, p], to[way])

    def row_first(p):
        for way in range(2):
            go(has[way], row_copy(way, r, 0, p))

    def row_step(j, p, h, way):
        z = (r - 1 - j) if way == 0 else (r + 1 + j)
        there = (z >= 0) & (z < NR)
        z = lax.rem(z + NR, NR)
        if j < NR - 2 and h == 0:
            sends.append((there & has[way], row_copy(way, z, j + 1, p)))

        @pl.when(there & (hop == h))
        def _():
            row_copy(way, z, j, p).wait_recv()
            if j < NR - 2:
                pl.when(has[way])(row_copy(way, z, j + 1, p).start)

    def chain_copy(t, p, src=None):
        return remote(pr.at[core, order[t], p], pc_send.at[t, p], pc_recv.at[t, p], (r, nxt), src)

    def back_copy(p, src=None):
        return remote(pr.at[core, order[3], p], pb_send.at[p], pc_recv.at[3, p], (r, prv), src)

    def sib_copy(t, p, src=None):
        return remote(pr.at[core, order[t], p], ps_send.at[t, p], ps_recv.at[t, p], (r, sib), src)

    def own_copy(t, p):
        z = order[t]
        return pltpu.make_async_copy(lt.at[z, p], pr.at[core, z, p], lc_sem.at[t, p])

    def chain(t, p, h):
        if h == 0:
            @pl.when(hop == 0)
            def _():
                src = lt.at[order[t], p]
                chain_copy(t, p, src).start()
                if t == 3:
                    back_copy(p, src).start()
                sib_copy(t, p, src).start()
                own_copy(t, p).start()
        else:
            @pl.when(hop == h)
            def _():
                chain_copy(t, p).wait_recv()
                if h < (2 if t == 3 else 3):
                    chain_copy(t, p).start()
                sib_copy(t, p).start()

    def split(t):
        z = lax.rem(r + t, NR)

        @pl.loop(0, NR)
        def _(kz):
            for side in range(2):
                a = decode(asl[side, kz, t, :rows], asl[side, kz, t, rows:])
                hi = a.astype(jnp.bfloat16)
                here = slice(side * 128, (side + 1) * 128)
                a_hi[kz, z, :, here] = hi
                a_lo[kz, z, :, here] = (a - hi.astype(jnp.float32)).astype(jnp.bfloat16)

    def product(p, ts):
        rhs = jnp.concatenate([lt[order[t], p] for t in ts] * 2, axis=1)
        lhs = jnp.concatenate([ref[order[t]].reshape(NR * rows, -1) for ref in (a_hi, a_lo) for t in ts], axis=1)
        return dot(lhs, rhs, ((1,), (1,))).reshape(NR, rows, wp)

    def panel_first(p):
        q_sum[p] = product(p, (0, 1, 2))

    def panel_last(p):
        total = q_sum[p] + product(p, (3,))
        for i in range(NR):
            part = jnp.where(structure[p // half, i] == 1, -total[i], 0.0)
            top = part.astype(jnp.bfloat16)
            q_hi[p, i] = top
            q_lo[p, i] = (part - top.astype(jnp.float32)).astype(jnp.bfloat16)

            @pl.when(i == r)
            def _():
                panel_out[:, p * wp:(p + 1) * wp] = part

    def arrived(t, p):
        pl.when(hop == 0)(own_copy(t, p).wait)
        remote(pr.at[1 - core, order[t], p], ps_send.at[t, p], ps_recv.at[t, p], (r, sib)).wait_recv()

    def subtract(k, part, count, p, ts):
        lhs = jnp.concatenate([pr[k, order[t], part:part + count].reshape(count * wp, rows) for t in ts] * 2, axis=1)
        rhs = jnp.concatenate([ref[p, order[t]] for ref in (q_hi, q_lo) for t in ts], axis=0)
        first = (k * half + part % half) * wp
        where = (slice(first, first + count * wp), slice(p * wp, (p + 1) * wp))
        diag_out[where] = diag_out[where] - dot(lhs, rhs, ((1,), (0,)))

    def update_first(p):
        for k in range(2):
            subtract(k, p // half * half, half, p, (0, 1, 2))

    def update_last(part):
        for k in range(2):
            for p in range(part // half * half, part // half * half + half):
                subtract(k, part, 1, p, (3,))

    steps = (tile_out, turn, chain, row_first, row_step, tiles_on, arrived, tiles_in, tiles_sib, split, panel_first, panel_last, update_first, update_last)
    for number, *args in ORDER:
        if number < 0:
            loads[3].wait()
        else:
            steps[number](*args)

    for cond, copy in sends:
        if cond is None:
            copy.wait_send()
        else:
            pl.when(cond)(copy.wait_send)
    for t in range(NR):
        for p in range(NP):
            pl.when(hop < (2 if t == 3 else 3))(chain_copy(t, p).wait_send)
            sib_copy(t, p).wait_send()
            if t == 3:
                pl.when(hop == 0)(back_copy(p).wait_send)


def idle(out):
    out[...] = jnp.zeros_like(out)


def write_out(panel, diag, panel_out, diag_out, sem):
    copies = [pltpu.make_async_copy(diag, diag_out, sem.at[0]), pltpu.make_async_copy(panel, panel_out, sem.at[1])]
    for copy in copies:
        copy.start()
    for copy in copies:
        copy.wait()


def local_kernel(factor_panel, ancestor_inv, diag_inverse, structure):
    rows, width = factor_panel.shape
    wp = width // NP
    acols = ancestor_inv.shape[1]
    dma = pltpu.SemaphoreType.DMA
    bf16, f32 = jnp.bfloat16, jnp.float32
    vmem = pl.BlockSpec(memory_space=pltpu.VMEM)
    anywhere = pl.BlockSpec(memory_space=pl.ANY)
    shapes = (
        jax.ShapeDtypeStruct((rows, width), f32),
        jax.ShapeDtypeStruct(diag_inverse.shape, f32),
    )
    opened = pl.pallas_call(
        idle,
        out_shape=jax.ShapeDtypeStruct((8, 128), f32),
        out_specs=vmem,
        cost_estimate=pl.CostEstimate(flops=8 << 30, bytes_accessed=1 << 12, transcendentals=0),
        compiler_params=pltpu.CompilerParams(has_side_effects=True, vmem_limit_bytes=16 << 20),
    )()
    panel, diag = pl.pallas_call(
        kernel,
        out_shape=shapes,
        in_specs=[anywhere] * 4 + [vmem],
        out_specs=(vmem, vmem),
        scratch_shapes=[
            pltpu.SMEM(structure.shape, jnp.int32),
            pltpu.VMEM((rows, width), bf16),
            pltpu.VMEM((rows, acols), f32),
            pltpu.VMEM((NR, NP, wp, rows), bf16),
            pltpu.VMEM((2, NR, NP, wp, rows), bf16),
            pltpu.VMEM((2, NC // 2, NR, rows + TAIL, acols), jnp.int16),
            pltpu.VMEM((NR, NR, rows, 2 * acols), bf16),
            pltpu.VMEM((NR, NR, rows, 2 * acols), bf16),
            pltpu.VMEM((NP, NR, rows, wp), f32),
            pltpu.VMEM((NP, NR, rows, wp), bf16),
            pltpu.VMEM((NP, NR, rows, wp), bf16),
            dma((2, NR - 1, NP)), dma((2, NR - 1, NP)), dma((NR - 1,)), dma((NR - 1,)),
            dma((2, 3)), dma((2, 3)), dma, dma,
            dma((NR, NP)), dma((NR, NP)), dma((NP,)), dma((NR, NP)), dma((NR, NP)),
            dma((NR, NP)), dma((4,)),
        ],
        compiler_params=pltpu.CompilerParams(
            collective_id=0, has_side_effects=True, vmem_limit_bytes=48 << 20),
    )(structure, factor_panel, ancestor_inv, diag_inverse, opened)
    return pl.pallas_call(
        write_out,
        out_shape=shapes,
        in_specs=[vmem, vmem],
        out_specs=(anywhere, anywhere),
        scratch_shapes=[dma((2,))],
        compiler_params=pltpu.CompilerParams(vmem_limit_bytes=40 << 20),
    )(panel, diag)


def solution(mesh):
    placed = (P("row", "col"), P("row", "col"), P("row", "col"), P())

    def body(factor_panel, ancestor_inv, diag_inverse, structure):
        rows, width = factor_panel.shape
        fits = (mesh.shape["row"], mesh.shape["col"]) == (NR, NC) and rows == B
        fits = fits and diag_inverse.shape[0] * NS == 2 * width
        return (local_kernel if fits else local)(factor_panel, ancestor_inv, diag_inverse, structure)

    return jax.shard_map(
        body,
        mesh=mesh,
        in_specs=placed,
        out_specs=(P("row", "col"), P("row", "col")),
        check_vma=False,
    )
```
